1024 devices in a mesh: section: 8 (over y_lo, x), seq: 128 (over y_hi, z, core).
Axes of the slice: x: 4, y: 8 (y_hi: 4, y_lo: 2; y = y_hi * 2 + y_lo), z: 16, core: 2. Of those that a mesh axis runs over, the one named last changes fastest.
Arguments:
- queries: bfloat16 [8, 16384, 4096], P('section', 'seq'), may hold values from -120 to 120
- grad_out: bfloat16 [8, 16384, 4096], P('section', 'seq'), may hold values from -6 to 6
- keys: bfloat16 [16384, 1024], P('seq', 'section'), may hold values from -5.5 to 5.5
- values: bfloat16 [16384, 1024], P('seq', 'section'), may hold values from -6 to 6
- key_first: int32 [128], P('seq'), may hold values from 0 to 127, as said below
Outputs:
- grad_queries: bfloat16 [8, 16384, 4096], P('section', 'seq')
- grad_keys: float32 [16384, 1024], P('seq', 'section')
- grad_values: float32 [16384, 1024], P('seq', 'section')
The draws below stay inside these ranges and needn't reach their ends.
Inputs may be any that keep to these rules, and one draw needn't show every extreme that they name: s - 1 <= key_first[s] <= s and key_first[s] >= 0; in every draw some shard s >= 1 has key_first[s] = s - 1.
All inputs are finite; a program needn't handle non-finite values.
Results may differ from the reference program's by a relative error of at most 0.008.
Values may be sent and summed in bfloat16 or wider, within the bound.
A program may use at most 64 MiB of HBM per device.

```python
import math
import jax
import jax.numpy as jnp
from jax import lax

HEADS = 32
KV_HEADS = 8
HEAD_DIM = 128
TQ = 128
SPAN = 2
SHARDS = 128
LAYERS = 8
NTOK = 16384
Q_WIDTH = 4096
KV_WIDTH = 1024


def cache_rows(key):
    kv_width = KV_HEADS * HEAD_DIM
    drawn = jnp.clip(jax.random.normal(jax.random.fold_in(key, 11), (NTOK, kv_width), jnp.float32), -5.0, 5.0)
    return drawn


def draw_keys(key, part):
    return cache_rows(key).astype(jnp.bfloat16)


def draw_queries(key, part):
    q_width = HEADS * HEAD_DIM
    drawn = jnp.clip(jax.random.normal(jax.random.fold_in(key, 21), (LAYERS, NTOK, q_width), jnp.float32), -5.0, 5.0)
    return drawn.astype(jnp.bfloat16)


def draw_key_first(key, part):
    shard_ids = jnp.arange(SHARDS, dtype=jnp.int32)
    reach_back = jax.random.randint(jax.random.fold_in(key, 31), (SHARDS,), 0, SPAN)
    chosen = jax.random.randint(jax.random.fold_in(key, 32), (), SPAN - 1, SHARDS)
    reach_back = jnp.where(shard_ids == chosen, SPAN - 1, reach_back)
    return jnp.maximum(shard_ids - reach_back, 0).astype(jnp.int32)


def level_of(own_key, dims, cuts, least, top_value):
    gain = 1.0
    for dim, parts in cuts:
        steps = jax.random.uniform(jax.random.fold_in(jax.random.fold_in(own_key, 6), dim), (parts,), jnp.float32, least / len(cuts), top_value / len(cuts))
        gain = gain * jnp.repeat(jnp.exp(steps), dims[dim] // parts).reshape((-1,) + (1,) * (len(dims) - 1 - dim))
    return gain


def scatter_about(key, dims, scale, bound, cuts=(), held_as=jnp.bfloat16):
    drawn = jax.random.normal(key, dims, jnp.float32) * scale
    if len(cuts) > 0:
        drawn = level_of(key, dims, cuts, -0.22, 0.18) * drawn
    return jnp.clip(drawn, min=-bound, max=bound).astype(held_as)


def setup_inputs(seed: int = 0) -> dict:
    key_of = jax.random.split(jax.random.key(seed), 6)
    return {
        "queries": draw_queries(jax.random.fold_in(key_of[5], 71), 0),
        "grad_out": scatter_about(key_of[1], (LAYERS, NTOK, Q_WIDTH), 1.0, 6.0, ((0, 8), (1, 128))),
        "keys": draw_keys(jax.random.fold_in(key_of[5], 71), 0),
        "values": scatter_about(key_of[3], (NTOK, KV_WIDTH), 1.0, 6.0, ((0, 128), (1, 8))),
        "key_first": draw_key_first(jax.random.fold_in(key_of[5], 71), 0),
    }


masked_score = -1e+30

def shard_grads(query_rows, grad_rows, key_win, value_win, key_start, shard_index):
    group_size = HEADS // KV_HEADS
    key_count = SPAN * TQ
    score_scale = 1.0 / math.sqrt(HEAD_DIM)
    q_float = query_rows.astype(jnp.float32).reshape(TQ, KV_HEADS, group_size, HEAD_DIM)
    g_float = grad_rows.astype(jnp.float32).reshape(TQ, KV_HEADS, group_size, HEAD_DIM)
    k_float = key_win.astype(jnp.float32).reshape(key_count, KV_HEADS, HEAD_DIM)
    v_float = value_win.astype(jnp.float32).reshape(key_count, KV_HEADS, HEAD_DIM)
    q_pos = shard_index * TQ + jnp.arange(TQ, dtype=jnp.int32)
    k_pos = (shard_index - SPAN + 1) * TQ + jnp.arange(key_count, dtype=jnp.int32)
    visible = (k_pos[None, :] >= key_start * TQ) & (k_pos[None, :] <= q_pos[:, None])
    scores = jnp.einsum('ikgd,tkd->kgit', q_float, k_float) * score_scale
    scores = jnp.where(visible, scores, masked_score)
    row_max = lax.optimization_barrier(jnp.max(scores, axis=-1, keepdims=True))
    weights = jnp.exp(scores - row_max)
    weights = weights / lax.optimization_barrier(jnp.sum(weights, axis=-1, keepdims=True))
    dprob = jnp.einsum('ikgd,tkd->kgit', g_float, v_float)
    row_dot = lax.optimization_barrier(jnp.sum(weights * dprob, axis=-1, keepdims=True))
    dscore = (weights * (dprob - row_dot) * score_scale).astype(jnp.bfloat16)
    wround = weights.astype(jnp.bfloat16)
    dscore, wround = lax.optimization_barrier((dscore, wround))
    ds_float = dscore.astype(jnp.float32)
    w_float = wround.astype(jnp.float32)
    grad_q = jnp.einsum('kgit,tkd->ikgd', ds_float, k_float).reshape(TQ, HEADS * HEAD_DIM).astype(jnp.bfloat16)
    grad_k = jnp.einsum('kgit,ikgd->tkd', ds_float, q_float).reshape(key_count, KV_HEADS * HEAD_DIM)
    grad_v = jnp.einsum('kgit,ikgd->tkd', w_float, g_float).reshape(key_count, KV_HEADS * HEAD_DIM)
    return (grad_q, grad_k, grad_v)

def reference(queries, grad_out, keys, values, key_first):
    kv_width = KV_HEADS * HEAD_DIM
    zero_rows = jnp.zeros(((SPAN - 1) * TQ, kv_width), keys.dtype)
    keys_pad = jnp.concatenate([zero_rows, keys], axis=0)
    values_pad = jnp.concatenate([zero_rows, values], axis=0)

    def per_layer(running, layer_in):
        q_layer, g_layer = layer_in

        def per_shard(shard_index):
            start = shard_index * TQ
            q_rows = lax.dynamic_slice_in_dim(q_layer, start, TQ, 0)
            g_rows = lax.dynamic_slice_in_dim(g_layer, start, TQ, 0)
            key_win = lax.dynamic_slice_in_dim(keys_pad, start, SPAN * TQ, 0)
            value_win = lax.dynamic_slice_in_dim(values_pad, start, SPAN * TQ, 0)
            key_start = lax.dynamic_index_in_dim(key_first, shard_index, 0, keepdims=False)
            return shard_grads(q_rows, g_rows, key_win, value_win, key_start, shard_index)
        grad_q, grad_k, grad_v = lax.map(per_shard, jnp.arange(SHARDS, dtype=jnp.int32))
        return ((running[0] + grad_k, running[1] + grad_v), grad_q.reshape(NTOK, HEADS * HEAD_DIM))
    zero_acc = jnp.zeros((SHARDS, SPAN * TQ, kv_width), jnp.float32)
    (key_wins, value_wins), grad_queries = lax.scan(per_layer, (zero_acc, zero_acc), (queries, grad_out))
    key_wins = key_wins.reshape(SHARDS, SPAN, TQ, kv_width)
    value_wins = value_wins.reshape(SHARDS, SPAN, TQ, kv_width)
    summed_k = jnp.zeros((SHARDS + SPAN - 1, TQ, kv_width), jnp.float32)
    summed_v = jnp.zeros((SHARDS + SPAN - 1, TQ, kv_width), jnp.float32)
    for window_slot in range(SPAN):
        summed_k = summed_k.at[window_slot:window_slot + SHARDS].add(key_wins[:, window_slot])
        summed_v = summed_v.at[window_slot:window_slot + SHARDS].add(value_wins[:, window_slot])
    grad_keys = summed_k[SPAN - 1:].reshape(NTOK, kv_width)
    grad_values = summed_v[SPAN - 1:].reshape(NTOK, kv_width)
    return (grad_queries, grad_keys, grad_values)
```

```python
import math

import jax
import jax.numpy as jnp
from jax import lax
from jax.experimental import pallas as pl
from jax.experimental.pallas import tpu as pltpu
from jax.sharding import PartitionSpec as P

KV_HEADS = 8
GROUP = 4
HEAD_DIM = 128
TQ = 128
GROUP_WIDTH = GROUP * HEAD_DIM
MESH = pl.DeviceIdType.MESH

OFFSETS = ((0, 0), (1, 0), (0, 1), (0, 3), (1, 1), (1, 3), (0, 2), (1, 2))
AHEAD = 2
LAG = 2
HEADS_AT_ONCE = 2

masked_score = -1e30
never = 1e30


def dot(a, b, contract):
    return lax.dot_general(a, b, ((contract[:1], contract[1:]), ((), ())), preferred_element_type=jnp.float32)


def kernel(
    q_hbm, g_hbm, k_hbm, v_hbm, first_hbm,
    dq_ref, dk_ref, dv_ref,
    q_buf, g_buf, cur, prev, acc, back_out, back_in, part_out, part_in, first,
    q_sem, g_sem, own_sem, first_sem,
    cur_send, cur_recv, prev_send, prev_recv, back_send, back_recv, part_send, part_recv,
):
    section = lax.axis_index("section")
    shard = lax.axis_index("seq")
    shards = lax.axis_size("seq")
    y, x = section // 4, section % 4
    heads = [((y + dy) % 2) * 4 + (x + dx) % 4 for dy, dx in OFFSETS]
    askers = [((y + dy) % 2) * 4 + (x + 4 - dx) % 4 for dy, dx in OFFSETS]
    later = (shard + 1) % shards
    earlier = (shard + shards - 1) % shards
    steps = range(KV_HEADS)

    def columns(j):
        return pl.ds(pl.multiple_of(heads[j] * GROUP_WIDTH, GROUP_WIDTH), GROUP_WIDTH)

    own = [
        pltpu.make_async_copy(k_hbm, cur.at[0, 0], own_sem.at[0]),
        pltpu.make_async_copy(v_hbm, cur.at[0, 1], own_sem.at[1]),
    ]
    first_copy = pltpu.make_async_copy(first_hbm, first, first_sem)
    q_copies = [pltpu.make_async_copy(q_hbm.at[0, :, columns(j)], q_buf.at[j], q_sem.at[j]) for j in steps]
    g_copies = [pltpu.make_async_copy(g_hbm.at[0, :, columns(j)], g_buf.at[j], g_sem.at[j]) for j in steps]
    for copy in own:
        copy.start()
    first_copy.start()
    for j in steps:
        q_copies[j].start()
        g_copies[j].start()

    def remote(src, dst, send, recv, section_to, shard_to):
        return pltpu.make_async_remote_copy(
            src_ref=src, dst_ref=dst, send_sem=send, recv_sem=recv,
            device_id=(section_to, shard_to), device_id_type=MESH,
        )

    gathers = [remote(cur.at[0], cur.at[j], cur_send.at[j], cur_recv.at[j], askers[j], shard) for j in steps[1:]]
    gathers = [None] + gathers
    forwards = [remote(cur.at[j], prev.at[j], prev_send.at[j], prev_recv.at[j], section, later) for j in steps]
    backs = [remote(back_out.at[j], back_in.at[j], back_send.at[j], back_recv.at[j], section, earlier) for j in steps]
    parts = [remote(part_out.at[j], part_in.at[j], part_send.at[j], part_recv.at[j], heads[j], shard) for j in steps[1:]]
    parts = [None] + parts

    barrier = pltpu.get_barrier_semaphore()
    for j in steps[1:]:
        pl.semaphore_signal(barrier, inc=1, device_id=(heads[j], shard), device_id_type=MESH)
    for near in (earlier, later):
        pl.semaphore_signal(barrier, inc=1, device_id=(section, near), device_id_type=MESH)
    pl.semaphore_wait(barrier, KV_HEADS - 1 + 2)

    for copy in own:
        copy.wait()
    forwards[0].start()
    for j in steps[1:]:
        gathers[j].start()
    first_copy.wait()
    sees_earlier = first[0] < shard

    score_scale = 1.0 / math.sqrt(HEAD_DIM)
    base2_scale = score_scale * math.log2(math.e)
    key_pos = lax.broadcasted_iota(jnp.int32, (TQ, TQ), 0)
    query_pos = lax.broadcasted_iota(jnp.int32, (TQ, TQ), 1)
    causal = key_pos <= query_pos
    causal = jnp.concatenate([causal] * HEADS_AT_ONCE, axis=1)

    def compute(j):
        k_win = jnp.concatenate([prev[j, 0], cur[j, 0]], axis=0)
        v_win = jnp.concatenate([prev[j, 1], cur[j, 1]], axis=0)
        dk = dv = None
        for low in range(0, GROUP, HEADS_AT_ONCE):
            lanes = [slice(a * HEAD_DIM, (a + 1) * HEAD_DIM) for a in range(low, low + HEADS_AT_ONCE)]
            q = jnp.concatenate([q_buf[j, :, lane] for lane in lanes], axis=0)
            g = jnp.concatenate([g_buf[j, :, lane] for lane in lanes], axis=0)
            scores = dot(k_win, q, (1, 1))
            dprob = dot(v_win, g, (1, 1))
            old, new = scores[:TQ], jnp.where(causal, scores[TQ:], masked_score)
            old_max = jnp.where(sees_earlier, jnp.max(old, axis=0, keepdims=True), masked_score)
            row_max = jnp.maximum(old_max, jnp.max(new, axis=0, keepdims=True))
            old_shift = jnp.where(sees_earlier, row_max, never)
            powers = jnp.concatenate(
                [jnp.exp2((old - old_shift) * base2_scale), jnp.exp2((new - row_max) * base2_scale)], axis=0
            )
            inverse = 1.0 / jnp.sum(powers, axis=0, keepdims=True)
            weights = powers * inverse
            row_dot = jnp.sum(weights * dprob, axis=0, keepdims=True)
            dscore = (weights * ((dprob - row_dot) * score_scale)).astype(jnp.bfloat16)
            wround = weights.astype(jnp.bfloat16)
            dk_part, dv_part = dot(dscore, q, (1, 0)), dot(wround, g, (1, 0))
            dk = dk_part if dk is None else dk + dk_part
            dv = dv_part if dv is None else dv + dv_part
            dq = dot(dscore, k_win, (0, 0)).astype(jnp.bfloat16)
            for n in range(HEADS_AT_ONCE):
                at = pl.multiple_of(heads[j] * GROUP_WIDTH + (low + n) * HEAD_DIM, HEAD_DIM)
                dq_ref[0, :, pl.ds(at, HEAD_DIM)] = dq[n * TQ : (n + 1) * TQ]
        back_out[j, 0] = dk[:TQ].astype(jnp.bfloat16)
        back_out[j, 1] = dv[:TQ].astype(jnp.bfloat16)
        backs[j].start()
        acc[j, 0] = dk[TQ:]
        acc[j, 1] = dv[TQ:]

    def finish(j):
        backs[j].wait_recv()
        total = acc[j] + back_in[j].astype(jnp.float32)
        if j == 0:
            acc[j] = total
        else:
            part_out[j] = total.astype(jnp.bfloat16)
            parts[j].start()

    def pass_on(j):
        gathers[j].wait_recv()
        forwards[j].start()

    for j in range(1, AHEAD):
        pass_on(j)
    for j in steps:
        if j + AHEAD < KV_HEADS:
            pass_on(j + AHEAD)
        forwards[j].wait_recv()
        q_copies[j].wait()
        g_copies[j].wait()
        compute(j)
        if j >= LAG:
            finish(j - LAG)
    for j in range(KV_HEADS - LAG, KV_HEADS):
        finish(j)

    total = acc[0]
    for j in steps[1:]:
        parts[j].wait_recv()
        total = total + part_in[j].astype(jnp.float32)
    dk_ref[...] = total[0]
    dv_ref[...] = total[1]

    for j in steps:
        forwards[j].wait_send()
        backs[j].wait_send()
        if j > 0:
            gathers[j].wait_send()
            parts[j].wait_send()


def body(queries, grad_out, keys, values, key_first):
    rows, width = queries.shape[1:]
    block = (KV_HEADS, 2, TQ, HEAD_DIM)
    group = (KV_HEADS, rows, GROUP_WIDTH)
    pairs = math.prod((KV_HEADS, GROUP, TQ, 2 * TQ))
    return pl.pallas_call(
        kernel,
        out_shape=(
            jax.ShapeDtypeStruct(queries.shape, jnp.bfloat16),
            jax.ShapeDtypeStruct(keys.shape, jnp.float32),
            jax.ShapeDtypeStruct(values.shape, jnp.float32),
        ),
        in_specs=[pl.BlockSpec(memory_space=pltpu.HBM)] * 5,
        out_specs=[pl.BlockSpec(memory_space=pltpu.VMEM)] * 3,
        scratch_shapes=[
            pltpu.VMEM(group, jnp.bfloat16),
            pltpu.VMEM(group, jnp.bfloat16),
            pltpu.VMEM(block, jnp.bfloat16),
            pltpu.VMEM(block, jnp.bfloat16),
            pltpu.VMEM(block, jnp.float32),
            pltpu.VMEM(block, jnp.bfloat16),
            pltpu.VMEM(block, jnp.bfloat16),
            pltpu.VMEM(block, jnp.bfloat16),
            pltpu.VMEM(block, jnp.bfloat16),
            pltpu.SMEM((1,), jnp.int32),
            pltpu.SemaphoreType.DMA((KV_HEADS,)),
            pltpu.SemaphoreType.DMA((KV_HEADS,)),
            pltpu.SemaphoreType.DMA((2,)),
            pltpu.SemaphoreType.DMA,
        ]
        + [pltpu.SemaphoreType.DMA((KV_HEADS,))] * 8,
        compiler_params=pltpu.CompilerParams(
            collective_id=0, has_side_effects=True, vmem_limit_bytes=62 * 2**20
        ),
        cost_estimate=pl.CostEstimate(
            flops=10 * pairs * HEAD_DIM, transcendentals=pairs, bytes_accessed=3 * 2 * rows * width
        ),
    )(queries, grad_out, keys, values, key_first)


def solution(mesh):
    placed = (
        P("section", "seq", None),
        P("section", "seq", None),
        P("seq", "section"),
        P("seq", "section"),
        P("seq"),
    )
    return jax.shard_map(
        body,
        mesh=mesh,
        in_specs=placed,
        out_specs=(P("section", "seq", None), P("seq", "section"), P("seq", "section")),
        check_vma=False,
    )
```

```python
import functools
import math

import jax
import jax.numpy as jnp
from jax import lax
from jax.experimental import pallas as pl
from jax.experimental.pallas import tpu as pltpu
from jax.sharding import PartitionSpec as P

KV_HEADS = 8
GROUP = 4
HEAD_DIM = 128
TQ = 128
GROUP_WIDTH = GROUP * HEAD_DIM
MESH = pl.DeviceIdType.MESH

OFFSETS = ((0, 0), (1, 0), (0, 1), (0, 3), (1, 1), (1, 3), (0, 2), (1, 2))
AHEAD = 2
LAG = 2
RUN = 32
HEADS_AT_ONCE = 4

masked_score = -1e30
never = 1e30


def dot(a, b, contract):
    return lax.dot_general(a, b, ((contract[:1], contract[1:]), ((), ())), preferred_element_type=jnp.float32)


def kernel(
    q_hbm, g_hbm, k_hbm, v_hbm, first_hbm,
    dq_ref, dk_ref, dv_ref,
    q_buf, g_buf, cur, prev, acc, back_out, back_in, part_out, part_in,
    edge_in, edge_out, edge_last, first,
    q_sem, g_sem, own_sem, first_sem,
    cur_send, cur_recv, forward_send, relay_send, prev_recv, back_send, back_recv, part_send, part_recv,
    edge_send, edge_recv,
):
    section = lax.axis_index("section")
    shard = lax.axis_index("seq")
    shards = lax.axis_size("seq")
    y, x = section // 4, section % 4
    heads = [((y + dy) % 2) * 4 + (x + dx) % 4 for dy, dx in OFFSETS]
    askers = [((y + dy) % 2) * 4 + (x + 4 - dx) % 4 for dy, dx in OFFSETS]
    later = (shard + 1) % shards
    near_earlier = shard % RUN != 0
    near_later = (shard + 1) % RUN != 0
    has_earlier = shard > 0
    has_later = shard < shards - 1
    far_earlier = jnp.logical_and(has_earlier, jnp.logical_not(near_earlier))
    far_later = jnp.logical_and(has_later, jnp.logical_not(near_later))
    run_start = jnp.logical_not(near_earlier)
    earlier = (shard + shards - 1) % shards
    steps = range(KV_HEADS)

    def columns(j):
        return pl.ds(pl.multiple_of(heads[j] * GROUP_WIDTH, GROUP_WIDTH), GROUP_WIDTH)

    own = [
        pltpu.make_async_copy(k_hbm, cur.at[0, 0], own_sem.at[0]),
        pltpu.make_async_copy(v_hbm, cur.at[0, 1], own_sem.at[1]),
    ]
    first_copy = pltpu.make_async_copy(first_hbm, first, first_sem)
    q_copies = [pltpu.make_async_copy(q_hbm.at[0, :, columns(j)], q_buf.at[j], q_sem.at[j]) for j in steps]
    g_copies = [pltpu.make_async_copy(g_hbm.at[0, :, columns(j)], g_buf.at[j], g_sem.at[j]) for j in steps]
    for copy in own:
        copy.start()

    def remote(src, dst, send, recv, section_to, shard_to):
        return pltpu.make_async_remote_copy(
            src_ref=src, dst_ref=dst, send_sem=send, recv_sem=recv,
            device_id=(section_to, shard_to), device_id_type=MESH,
        )

    gathers = [remote(cur.at[0], cur.at[j], cur_send.at[j], cur_recv.at[j], askers[j], shard) for j in steps[1:]]
    gathers = [None] + gathers
    forwards = [remote(cur.at[j], prev.at[j], forward_send.at[j], prev_recv.at[j], section, later) for j in steps]
    relays = [remote(prev.at[0], prev.at[j], relay_send.at[j], prev_recv.at[j], askers[j], shard) for j in steps[1:]]
    relays = [None] + relays
    backs = [remote(back_out.at[j], back_in.at[j], back_send.at[j], back_recv.at[j], section, earlier) for j in steps]
    parts = [remote(part_out.at[j], part_in.at[j], part_send.at[j], part_recv.at[j], heads[j], shard) for j in steps[1:]]
    parts = [None] + parts
    edges = [remote(back_out.at[j], edge_in.at[j], edge_send.at[j], edge_recv.at[j], heads[j], shard) for j in steps[1:]]
    edges = [remote(edge_out, edge_last, edge_send.at[0], edge_recv.at[0], section, earlier)] + edges

    barrier = pltpu.get_barrier_semaphore()
    for j in steps[1:]:
        pl.semaphore_signal(barrier, inc=1, device_id=(heads[j], shard), device_id_type=MESH)

    @pl.when(has_earlier)
    def _():
        pl.semaphore_signal(barrier, inc=1, device_id=(section, earlier), device_id_type=MESH)

    pl.semaphore_wait(barrier, KV_HEADS - 1 + jnp.where(has_later, 1, 0))

    for copy in own:
        copy.wait()
    pl.when(has_later)(forwards[0].start)
    pl.when(far_later)(forwards[0].wait_send)
    for j in steps[1:]:
        gathers[j].start()
    first_copy.start()
    for j in steps:
        q_copies[j].start()
        g_copies[j].start()
    first_copy.wait()
    sees_earlier = first[0] < shard

    score_scale = 1.0 / math.sqrt(HEAD_DIM)
    base2_scale = score_scale * math.log2(math.e)
    key_pos = lax.broadcasted_iota(jnp.int32, (TQ, TQ), 0)
    query_pos = lax.broadcasted_iota(jnp.int32, (TQ, TQ), 1)
    causal = key_pos <= query_pos
    causal = jnp.concatenate([causal] * HEADS_AT_ONCE, axis=1)

    def compute(j):
        k_win = jnp.concatenate([prev[j, 0], cur[j, 0]], axis=0)
        v_win = jnp.concatenate([prev[j, 1], cur[j, 1]], axis=0)
        dk = dv = None
        for low in range(0, GROUP, HEADS_AT_ONCE):
            lanes = [slice(a * HEAD_DIM, (a + 1) * HEAD_DIM) for a in range(low, low + HEADS_AT_ONCE)]
            q = jnp.concatenate([q_buf[j, :, lane] for lane in lanes], axis=0)
            g = jnp.concatenate([g_buf[j, :, lane] for lane in lanes], axis=0)
            scores = dot(k_win, q, (1, 1))
            dprob = dot(v_win, g, (1, 1))
            old, new = scores[:TQ], jnp.where(causal, scores[TQ:], masked_score)
            old_max = jnp.where(sees_earlier, jnp.max(old, axis=0, keepdims=True), masked_score)
            row_max = jnp.maximum(old_max, jnp.max(new, axis=0, keepdims=True))
            old_shift = jnp.where(sees_earlier, row_max, never)
            powers = jnp.concatenate(
                [jnp.exp2((old - old_shift) * base2_scale), jnp.exp2((new - row_max) * base2_scale)], axis=0
            )
            inverse = 1.0 / jnp.sum(powers, axis=0, keepdims=True)
            weights = powers * inverse
            row_dot = jnp.sum(weights * dprob, axis=0, keepdims=True)
            dscore = (weights * ((dprob - row_dot) * score_scale)).astype(jnp.bfloat16)
            wround = weights.astype(jnp.bfloat16)
            dk_part, dv_part = dot(dscore, q, (1, 0)), dot(wround, g, (1, 0))
            dk = dk_part if dk is None else dk + dk_part
            dv = dv_part if dv is None else dv + dv_part
            dq = dot(dscore, k_win, (0, 0)).astype(jnp.bfloat16)
            for n in range(HEADS_AT_ONCE):
                at = pl.multiple_of(heads[j] * GROUP_WIDTH + (low + n) * HEAD_DIM, HEAD_DIM)
                dq_ref[0, :, pl.ds(at, HEAD_DIM)] = dq[n * TQ : (n + 1) * TQ]
        back_out[j, 0] = dk[:TQ].astype(jnp.bfloat16)
        back_out[j, 1] = dv[:TQ].astype(jnp.bfloat16)
        pl.when(near_earlier)(backs[j].start)
        if j > 0:
            pl.when(far_earlier)(edges[j].start)
        acc[j, 0] = dk[TQ:]
        acc[j, 1] = dv[TQ:]

    def finish(j):
        @pl.when(near_later)
        def _():
            backs[j].wait_recv()
            acc[j] += back_in[j].astype(jnp.float32)

        if j > 0:
            part_out[j] = acc[j].astype(jnp.bfloat16)
            parts[j].start()

    def pass_on(j):
        gathers[j].wait_recv()
        pl.when(near_later)(forwards[j].start)

    @pl.when(run_start)
    def _():
        for j in steps[1:]:
            pass_on(j)

    @pl.when(jnp.logical_not(has_earlier))
    def _():
        prev[...] = jnp.zeros_like(prev)

    @pl.when(far_earlier)
    def _():
        forwards[0].wait_recv()
        for j in steps[1:]:
            relays[j].start()

    @pl.when(near_earlier)
    def _():
        for j in range(1, AHEAD):
            pass_on(j)
        forwards[0].wait_recv()

    for j in steps:
        if AHEAD <= j + AHEAD < KV_HEADS:
            pl.when(near_earlier)(functools.partial(pass_on, j + AHEAD))
        if j > 0:
            pl.when(has_earlier)(forwards[j].wait_recv)
        q_copies[j].wait()
        g_copies[j].wait()
        compute(j)
        pl.when(run_start)(functools.partial(finish, j))
        if j >= LAG:
            pl.when(near_earlier)(functools.partial(finish, j - LAG))
    for j in range(KV_HEADS - LAG, KV_HEADS):
        pl.when(near_earlier)(functools.partial(finish, j))

    @pl.when(far_earlier)
    def _():
        total = back_out[0].astype(jnp.float32)
        for j in steps[1:]:
            edges[j].wait_recv()
            total = total + edge_in[j].astype(jnp.float32)
        edge_out[...] = total.astype(jnp.bfloat16)
        edges[0].start()

    total = acc[0]
    for j in steps[1:]:
        parts[j].wait_recv()
        total = total + part_in[j].astype(jnp.float32)
    dk_ref[...] = total[0]
    dv_ref[...] = total[1]

    @pl.when(far_later)
    def _():
        edges[0].wait_recv()
        dk_ref[...] += edge_last[0].astype(jnp.float32)
        dv_ref[...] += edge_last[1].astype(jnp.float32)

    pl.when(near_later)(forwards[0].wait_send)
    for j in steps:
        pl.when(near_earlier)(backs[j].wait_send)
        pl.when(far_earlier)(edges[j].wait_send)
        if j > 0:
            gathers[j].wait_send()
            parts[j].wait_send()
            pl.when(near_later)(forwards[j].wait_send)
            pl.when(far_earlier)(relays[j].wait_send)


def body(queries, grad_out, keys, values, key_first):
    rows, width = queries.shape[1:]
    block = (KV_HEADS, 2, TQ, HEAD_DIM)
    group = (KV_HEADS, rows, GROUP_WIDTH)
    pairs = math.prod((KV_HEADS, GROUP, TQ, 2 * TQ))
    return pl.pallas_call(
        kernel,
        out_shape=(
            jax.ShapeDtypeStruct(queries.shape, jnp.bfloat16),
            jax.ShapeDtypeStruct(keys.shape, jnp.float32),
            jax.ShapeDtypeStruct(values.shape, jnp.float32),
        ),
        in_specs=[pl.BlockSpec(memory_space=pltpu.HBM)] * 5,
        out_specs=[pl.BlockSpec(memory_space=pltpu.VMEM)] * 3,
        scratch_shapes=[
            pltpu.VMEM(group, jnp.bfloat16),
            pltpu.VMEM(group, jnp.bfloat16),
            pltpu.VMEM(block, jnp.bfloat16),
            pltpu.VMEM(block, jnp.bfloat16),
            pltpu.VMEM(block, jnp.float32),
            pltpu.VMEM(block, jnp.bfloat16),
            pltpu.VMEM(block, jnp.bfloat16),
            pltpu.VMEM(block, jnp.bfloat16),
            pltpu.VMEM(block, jnp.bfloat16),
            pltpu.VMEM(block, jnp.bfloat16),
            pltpu.VMEM(block[1:], jnp.bfloat16),
            pltpu.VMEM(block[1:], jnp.bfloat16),
            pltpu.SMEM((1,), jnp.int32),
            pltpu.SemaphoreType.DMA((KV_HEADS,)),
            pltpu.SemaphoreType.DMA((KV_HEADS,)),
            pltpu.SemaphoreType.DMA((2,)),
            pltpu.SemaphoreType.DMA,
        ]
        + [pltpu.SemaphoreType.DMA((KV_HEADS,))] * 11,
        compiler_params=pltpu.CompilerParams(
            collective_id=0, has_side_effects=True, vmem_limit_bytes=52 * 2**20
        ),
        cost_estimate=pl.CostEstimate(
            flops=10 * pairs * HEAD_DIM, transcendentals=pairs, bytes_accessed=3 * 2 * rows * width
        ),
    )(queries, grad_out, keys, values, key_first)


def solution(mesh):
    placed = (
        P("section", "seq", None),
        P("section", "seq", None),
        P("seq", "section"),
        P("seq", "section"),
        P("seq"),
    )
    return jax.shard_map(
        body,
        mesh=mesh,
        in_specs=placed,
        out_specs=(P("section", "seq", None), P("seq", "section"), P("seq", "section")),
        check_vma=False,
    )
```

```python
import functools
import math

import jax
import jax.numpy as jnp
from jax import lax
from jax.experimental import pallas as pl
from jax.experimental.pallas import tpu as pltpu
from jax.sharding import PartitionSpec as P

KV_HEADS = 8
GROUP = 4
HEAD_DIM = 128
TQ = 128
GROUP_WIDTH = GROUP * HEAD_DIM
MESH = pl.DeviceIdType.MESH

OFFSETS = ((0, 0), (1, 0), (0, 1), (0, 3), (1, 1), (1, 3), (0, 2), (1, 2))
AHEAD = 2
LAG = 2
RUN = 32
DIRECT_FROM = 4
HEADS_AT_ONCE = 4

masked_score = -1e30
never = 1e30


def dot(a, b, contract):
    return lax.dot_general(a, b, ((contract[:1], contract[1:]), ((), ())), preferred_element_type=jnp.float32)


def kernel(
    q_hbm, g_hbm, k_hbm, v_hbm, first_hbm,
    dq_ref, dkv_ref,
    q_buf, g_buf, cur, prev, acc, back_out, back_in, part_out, part_in,
    edge_in, edge_out, edge_last, first,
    q_sem, g_sem, own_sem, first_sem,
    cur_send, cur_recv, forward_send, relay_send, prev_recv, back_send, back_recv, part_send, part_recv,
    edge_send, edge_recv,
):
    section = lax.axis_index("section")
    shard = lax.axis_index("seq")
    shards = lax.axis_size("seq")
    y, x = section // 4, section % 4
    heads = [((y + dy) % 2) * 4 + (x + dx) % 4 for dy, dx in OFFSETS]
    askers = [((y + dy) % 2) * 4 + (x + 4 - dx) % 4 for dy, dx in OFFSETS]
    later = (shard + 1) % shards
    near_earlier = shard % RUN != 0
    near_later = (shard + 1) % RUN != 0
    has_earlier = shard > 0
    has_later = shard < shards - 1
    far_earlier = jnp.logical_and(has_earlier, jnp.logical_not(near_earlier))
    far_later = jnp.logical_and(has_later, jnp.logical_not(near_later))
    eager = shard % RUN < 2
    steady = jnp.logical_not(eager)
    earlier = (shard + shards - 1) % shards
    steps = range(KV_HEADS)

    def columns(j):
        return pl.ds(pl.multiple_of(heads[j] * GROUP_WIDTH, GROUP_WIDTH), GROUP_WIDTH)

    own = [
        pltpu.make_async_copy(k_hbm, cur.at[0, 0], own_sem.at[0]),
        pltpu.make_async_copy(v_hbm, cur.at[0, 1], own_sem.at[1]),
    ]
    first_copy = pltpu.make_async_copy(first_hbm, first, first_sem)
    q_copies = [pltpu.make_async_copy(q_hbm.at[0, :, columns(j)], q_buf.at[j], q_sem.at[j]) for j in steps]
    g_copies = [pltpu.make_async_copy(g_hbm.at[0, :, columns(j)], g_buf.at[j], g_sem.at[j]) for j in steps]
    for copy in own:
        copy.start()

    def remote(src, dst, send, recv, section_to, shard_to):
        return pltpu.make_async_remote_copy(
            src_ref=src, dst_ref=dst, send_sem=send, recv_sem=recv,
            device_id=(section_to, shard_to), device_id_type=MESH,
        )

    gathers = [remote(cur.at[0], cur.at[j], cur_send.at[j], cur_recv.at[j], askers[j], shard) for j in steps[1:]]
    gathers = [None] + gathers
    forwards = [remote(cur.at[j], prev.at[j], forward_send.at[j], prev_recv.at[j], section, later) for j in steps]
    relays = [remote(prev.at[0], prev.at[j], relay_send.at[j], prev_recv.at[j], askers[j], shard) for j in steps[1:]]
    relays = [None] + relays
    backs = [remote(back_out.at[j], back_in.at[j], back_send.at[j], back_recv.at[j], section, earlier) for j in steps]
    parts = [remote(part_out.at[j], part_in.at[j], part_send.at[j], part_recv.at[j], heads[j], shard) for j in steps[1:]]
    parts = [None] + parts
    edges = [remote(back_out.at[j], edge_in.at[j], edge_send.at[j], edge_recv.at[j], heads[j], shard) for j in steps[1:]]
    edges = [remote(edge_out, edge_last, edge_send.at[0], edge_recv.at[0], section, earlier)] + edges

    barrier = pltpu.get_barrier_semaphore()
    for j in steps[1:]:
        pl.semaphore_signal(barrier, inc=1, device_id=(heads[j], shard), device_id_type=MESH)

    @pl.when(has_earlier)
    def _():
        pl.semaphore_signal(barrier, inc=1, device_id=(section, earlier), device_id_type=MESH)

    pl.semaphore_wait(barrier, KV_HEADS - 1 + jnp.where(has_later, 1, 0))

    for copy in own:
        copy.wait()
    pl.when(has_later)(forwards[0].start)
    pl.when(far_later)(forwards[0].wait_send)
    for j in steps[1:]:
        gathers[j].start()
    first_copy.start()
    for j in steps:
        q_copies[j].start()
        g_copies[j].start()
    first_copy.wait()
    sees_earlier = first[0] < shard

    score_scale = 1.0 / math.sqrt(HEAD_DIM)
    base2_scale = score_scale * math.log2(math.e)
    key_pos = lax.broadcasted_iota(jnp.int32, (TQ, TQ), 0)
    query_pos = lax.broadcasted_iota(jnp.int32, (TQ, TQ), 1)
    causal = key_pos <= query_pos
    causal = jnp.concatenate([causal] * HEADS_AT_ONCE, axis=1)

    def compute(j):
        k_win = jnp.concatenate([prev[j, 0], cur[j, 0]], axis=0)
        v_win = jnp.concatenate([prev[j, 1], cur[j, 1]], axis=0)
        dk = dv = None
        for low in range(0, GROUP, HEADS_AT_ONCE):
            lanes = [slice(a * HEAD_DIM, (a + 1) * HEAD_DIM) for a in range(low, low + HEADS_AT_ONCE)]
            q = jnp.concatenate([q_buf[j, :, lane] for lane in lanes], axis=0)
            g = jnp.concatenate([g_buf[j, :, lane] for lane in lanes], axis=0)
            scores = dot(k_win, q, (1, 1))
            dprob = dot(v_win, g, (1, 1))
            old, new = scores[:TQ], jnp.where(causal, scores[TQ:], masked_score)
            old_max = jnp.where(sees_earlier, jnp.max(old, axis=0, keepdims=True), masked_score)
            row_max = jnp.maximum(old_max, jnp.max(new, axis=0, keepdims=True))
            old_shift = jnp.where(sees_earlier, row_max, never)
            powers = jnp.concatenate(
                [jnp.exp2((old - old_shift) * base2_scale), jnp.exp2((new - row_max) * base2_scale)], axis=0
            )
            inverse = 1.0 / jnp.sum(powers, axis=0, keepdims=True)
            weights = powers * inverse
            row_dot = jnp.sum(weights * dprob, axis=0, keepdims=True)
            dscore = (weights * ((dprob - row_dot) * score_scale)).astype(jnp.bfloat16)
            wround = weights.astype(jnp.bfloat16)
            dk_part, dv_part = dot(dscore, q, (1, 0)), dot(wround, g, (1, 0))
            dk = dk_part if dk is None else dk + dk_part
            dv = dv_part if dv is None else dv + dv_part
            dq = dot(dscore, k_win, (0, 0)).astype(jnp.bfloat16)
            for n in range(HEADS_AT_ONCE):
                at = pl.multiple_of(heads[j] * GROUP_WIDTH + (low + n) * HEAD_DIM, HEAD_DIM)
                dq_ref[0, :, pl.ds(at, HEAD_DIM)] = dq[n * TQ : (n + 1) * TQ]
        back_out[j, 0] = dk[:TQ].astype(jnp.bfloat16)
        back_out[j, 1] = dv[:TQ].astype(jnp.bfloat16)
        pl.when(near_earlier if j < DIRECT_FROM else has_earlier)(backs[j].start)
        if 0 < j < DIRECT_FROM:
            pl.when(far_earlier)(edges[j].start)
        acc[j, 0] = dk[TQ:]
        acc[j, 1] = dv[TQ:]

    def finish(j):
        @pl.when(near_later if j < DIRECT_FROM else has_later)
        def _():
            backs[j].wait_recv()
            acc[j] += back_in[j].astype(jnp.float32)

        if j > 0:
            part_out[j] = acc[j].astype(jnp.bfloat16)
            parts[j].start()

    def pass_on(j):
        gathers[j].wait_recv()
        pl.when(near_later)(forwards[j].start)

    @pl.when(eager)
    def _():
        for j in steps[1:]:
            pass_on(j)

    @pl.when(jnp.logical_not(has_earlier))
    def _():
        prev[...] = jnp.zeros_like(prev)

    @pl.when(far_earlier)
    def _():
        forwards[0].wait_recv()
        for j in steps[1:]:
            relays[j].start()

    @pl.when(steady)
    def _():
        for j in range(1, AHEAD):
            pass_on(j)

    pl.when(near_earlier)(forwards[0].wait_recv)

    for j in steps:
        if AHEAD <= j + AHEAD < KV_HEADS:
            pl.when(steady)(functools.partial(pass_on, j + AHEAD))
        if j > 0:
            pl.when(has_earlier)(forwards[j].wait_recv)
        q_copies[j].wait()
        g_copies[j].wait()
        compute(j)
        pl.when(eager)(functools.partial(finish, j))
        if j >= LAG:
            pl.when(steady)(functools.partial(finish, j - LAG))
    for j in range(KV_HEADS - LAG, KV_HEADS):
        pl.when(steady)(functools.partial(finish, j))

    @pl.when(far_earlier)
    def _():
        total = back_out[0].astype(jnp.float32)
        for j in range(1, DIRECT_FROM):
            edges[j].wait_recv()
            total = total + edge_in[j].astype(jnp.float32)
        edge_out[...] = total.astype(jnp.bfloat16)
        edges[0].start()

    total = acc[0]
    for j in steps[1:]:
        parts[j].wait_recv()
        total = total + part_in[j].astype(jnp.float32)
    dkv_ref[...] = total

    @pl.when(far_later)
    def _():
        edges[0].wait_recv()
        dkv_ref[...] += edge_last[...].astype(jnp.float32)

    pl.when(near_later)(forwards[0].wait_send)
    for j in steps:
        pl.when(near_earlier if j < DIRECT_FROM else has_earlier)(backs[j].wait_send)
        if j < DIRECT_FROM:
            pl.when(far_earlier)(edges[j].wait_send)
        if j > 0:
            gathers[j].wait_send()
            parts[j].wait_send()
            pl.when(near_later)(forwards[j].wait_send)
            pl.when(far_earlier)(relays[j].wait_send)


def body(queries, grad_out, keys, values, key_first):
    rows, width = queries.shape[1:]
    block = (KV_HEADS, 2, TQ, HEAD_DIM)
    group = (KV_HEADS, rows, GROUP_WIDTH)
    pairs = math.prod((KV_HEADS, GROUP, TQ, 2 * TQ))
    grad_queries, cache_grads = pl.pallas_call(
        kernel,
        out_shape=(
            pltpu.VMEM(queries.shape, jnp.bfloat16),
            pltpu.VMEM((2,) + keys.shape, jnp.float32),
        ),
        in_specs=[pl.BlockSpec(memory_space=pltpu.HBM)] * 5,
        out_specs=[pl.BlockSpec(memory_space=pltpu.VMEM)] * 2,
        scratch_shapes=[
            pltpu.VMEM(group, jnp.bfloat16),
            pltpu.VMEM(group, jnp.bfloat16),
            pltpu.VMEM(block, jnp.bfloat16),
            pltpu.VMEM(block, jnp.bfloat16),
            pltpu.VMEM(block, jnp.float32),
            pltpu.VMEM(block, jnp.bfloat16),
            pltpu.VMEM(block, jnp.bfloat16),
            pltpu.VMEM(block, jnp.bfloat16),
            pltpu.VMEM(block, jnp.bfloat16),
            pltpu.VMEM(block, jnp.bfloat16),
            pltpu.VMEM(block[1:], jnp.bfloat16),
            pltpu.VMEM(block[1:], jnp.bfloat16),
            pltpu.SMEM((1,), jnp.int32),
            pltpu.SemaphoreType.DMA((KV_HEADS,)),
            pltpu.SemaphoreType.DMA((KV_HEADS,)),
            pltpu.SemaphoreType.DMA((2,)),
            pltpu.SemaphoreType.DMA,
        ]
        + [pltpu.SemaphoreType.DMA((KV_HEADS,))] * 11,
        compiler_params=pltpu.CompilerParams(
            collective_id=0, has_side_effects=True, vmem_limit_bytes=56 * 2**20
        ),
        cost_estimate=pl.CostEstimate(
            flops=10 * pairs * HEAD_DIM, transcendentals=pairs, bytes_accessed=3 * 2 * rows * width
        ),
    )(queries, grad_out, keys, values, key_first)
    return grad_queries, cache_grads[0], cache_grads[1]


def solution(mesh):
    placed = (
        P("section", "seq", None),
        P("section", "seq", None),
        P("seq", "section"),
        P("seq", "section"),
        P("seq"),
    )
    return jax.shard_map(
        body,
        mesh=mesh,
        in_specs=placed,
        out_specs=(P("section", "seq", None), P("seq", "section"), P("seq", "section")),
        check_vma=False,
    )
```

```python
import functools
import math

import jax
import jax.numpy as jnp
from jax import lax
from jax.experimental import pallas as pl
from jax.experimental.pallas import tpu as pltpu
from jax.sharding import PartitionSpec as P

KV_HEADS = 8
GROUP = 4
HEAD_DIM = 128
TQ = 128
GROUP_WIDTH = GROUP * HEAD_DIM
MESH = pl.DeviceIdType.MESH

OFFSETS = ((0, 0), (1, 0), (0, 1), (0, 3), (1, 1), (1, 3), (0, 2), (1, 2))
AHEAD = 2
LAG = 2
RUN = 32
DIRECT_FROM = 4

masked_score = -1e30
never = 1e30


def dot(a, b, contract):
    return lax.dot_general(a, b, ((contract[:1], contract[1:]), ((), ())), preferred_element_type=jnp.float32)


def kernel(
    q_hbm, g_hbm, k_hbm, v_hbm, first_hbm,
    dq_ref, dkv_ref,
    q_buf, g_buf, cur, prev, acc, back_out, back_in, part_out, part_in,
    edge_in, edge_out, edge_last, own_powers, own_dprob, own_rows, first,
    q_sem, g_sem, own_sem, first_sem,
    cur_send, cur_recv, forward_send, relay_send, prev_recv, back_send, back_recv, part_send, part_recv,
    edge_send, edge_recv,
):
    section = lax.axis_index("section")
    shard = lax.axis_index("seq")
    shards = lax.axis_size("seq")
    y, x = section // 4, section % 4
    heads = [((y + dy) % 2) * 4 + (x + dx) % 4 for dy, dx in OFFSETS]
    askers = [((y + dy) % 2) * 4 + (x + 4 - dx) % 4 for dy, dx in OFFSETS]
    later = (shard + 1) % shards
    near_earlier = shard % RUN != 0
    near_later = (shard + 1) % RUN != 0
    has_earlier = shard > 0
    has_later = shard < shards - 1
    far_earlier = jnp.logical_and(has_earlier, jnp.logical_not(near_earlier))
    far_later = jnp.logical_and(has_later, jnp.logical_not(near_later))
    eager = shard % RUN < 2
    steady = jnp.logical_not(eager)
    earlier = (shard + shards - 1) % shards
    steps = range(KV_HEADS)

    def columns(j):
        return pl.ds(pl.multiple_of(heads[j] * GROUP_WIDTH, GROUP_WIDTH), GROUP_WIDTH)

    own = [
        pltpu.make_async_copy(k_hbm, cur.at[0, 0], own_sem.at[0]),
        pltpu.make_async_copy(v_hbm, cur.at[0, 1], own_sem.at[1]),
    ]
    first_copy = pltpu.make_async_copy(first_hbm, first, first_sem)
    q_copies = [pltpu.make_async_copy(q_hbm.at[0, :, columns(j)], q_buf.at[j], q_sem.at[j]) for j in steps]
    g_copies = [pltpu.make_async_copy(g_hbm.at[0, :, columns(j)], g_buf.at[j], g_sem.at[j]) for j in steps]
    for copy in own:
        copy.start()

    def remote(src, dst, send, recv, section_to, shard_to):
        return pltpu.make_async_remote_copy(
            src_ref=src, dst_ref=dst, send_sem=send, recv_sem=recv,
            device_id=(section_to, shard_to), device_id_type=MESH,
        )

    gathers = [remote(cur.at[0], cur.at[j], cur_send.at[j], cur_recv.at[j], askers[j], shard) for j in steps[1:]]
    gathers = [None] + gathers
    forwards = [remote(cur.at[j], prev.at[j], forward_send.at[j], prev_recv.at[j], section, later) for j in steps]
    relays = [remote(prev.at[0], prev.at[j], relay_send.at[j], prev_recv.at[j], askers[j], shard) for j in steps[1:]]
    relays = [None] + relays
    backs = [remote(back_out.at[j], back_in.at[j], back_send.at[j], back_recv.at[j], section, earlier) for j in steps]
    parts = [remote(part_out.at[j], part_in.at[j], part_send.at[j], part_recv.at[j], heads[j], shard) for j in steps[1:]]
    parts = [None] + parts
    edges = [remote(back_out.at[j], edge_in.at[j], edge_send.at[j], edge_recv.at[j], heads[j], shard) for j in steps[1:]]
    edges = [remote(edge_out, edge_last, edge_send.at[0], edge_recv.at[0], section, earlier)] + edges

    barrier = pltpu.get_barrier_semaphore()
    for j in steps[1:]:
        pl.semaphore_signal(barrier, inc=1, device_id=(heads[j], shard), device_id_type=MESH)

    @pl.when(has_earlier)
    def _():
        pl.semaphore_signal(barrier, inc=1, device_id=(section, earlier), device_id_type=MESH)

    pl.semaphore_wait(barrier, KV_HEADS - 1 + jnp.where(has_later, 1, 0))

    for copy in own:
        copy.wait()
    pl.when(has_later)(forwards[0].start)
    pl.when(far_later)(forwards[0].wait_send)
    for j in steps[1:]:
        gathers[j].start()
    first_copy.start()
    for j in steps:
        q_copies[j].start()
        g_copies[j].start()
    first_copy.wait()
    sees_earlier = first[0] < shard

    score_scale = 1.0 / math.sqrt(HEAD_DIM)
    base2_scale = score_scale * math.log2(math.e)
    key_pos = lax.broadcasted_iota(jnp.int32, (TQ, TQ), 0)
    query_pos = lax.broadcasted_iota(jnp.int32, (TQ, TQ), 1)
    causal = key_pos <= query_pos
    causal = jnp.concatenate([causal] * GROUP, axis=1)

    def stacked(ref):
        return jnp.concatenate([ref[:, a * HEAD_DIM : (a + 1) * HEAD_DIM] for a in range(GROUP)], axis=0)

    def powers_of(scores, shift):
        return jnp.exp2((scores - shift) * base2_scale)

    def column_sum(x):
        return jnp.sum(x, axis=0, keepdims=True)

    def own_block(j):
        q_copies[j].wait()
        g_copies[j].wait()
        scores = jnp.where(causal, dot(cur[j, 0], stacked(q_buf.at[j]), (1, 1)), masked_score)
        dprob = dot(cur[j, 1], stacked(g_buf.at[j]), (1, 1))
        row_max = jnp.max(scores, axis=0, keepdims=True)
        powers = powers_of(scores, row_max)
        own_powers[j] = powers
        own_dprob[j] = dprob
        own_rows[j, 0:1] = row_max
        own_rows[j, 1:2] = column_sum(powers)
        own_rows[j, 2:3] = column_sum(powers * dprob)

    def compute(j):
        k_win = jnp.concatenate([prev[j, 0], cur[j, 0]], axis=0)
        q, g = stacked(q_buf.at[j]), stacked(g_buf.at[j])
        old = dot(prev[j, 0], q, (1, 1))
        old_dprob = dot(prev[j, 1], g, (1, 1))
        own_max = own_rows[j, 0:1]
        old_max = jnp.where(sees_earlier, jnp.max(old, axis=0, keepdims=True), masked_score)
        row_max = jnp.maximum(old_max, own_max)
        old_powers = powers_of(old, jnp.where(sees_earlier, row_max, never))
        rescale = powers_of(own_max, row_max)
        inverse = 1.0 / (rescale * own_rows[j, 1:2] + column_sum(old_powers))
        row_dot = (rescale * own_rows[j, 2:3] + column_sum(old_powers * old_dprob)) * inverse
        weights = jnp.concatenate([old_powers * inverse, own_powers[j] * (rescale * inverse)], axis=0)
        dprob = jnp.concatenate([old_dprob, own_dprob[j]], axis=0)
        dscore = (weights * ((dprob - row_dot) * score_scale)).astype(jnp.bfloat16)
        wround = weights.astype(jnp.bfloat16)
        dk, dv = dot(dscore, q, (1, 0)), dot(wround, g, (1, 0))
        dq = dot(dscore, k_win, (0, 0)).astype(jnp.bfloat16)
        for n in range(GROUP):
            at = pl.multiple_of(heads[j] * GROUP_WIDTH + n * HEAD_DIM, HEAD_DIM)
            dq_ref[0, :, pl.ds(at, HEAD_DIM)] = dq[n * TQ : (n + 1) * TQ]
        back_out[j, 0] = dk[:TQ].astype(jnp.bfloat16)
        back_out[j, 1] = dv[:TQ].astype(jnp.bfloat16)
        pl.when(near_earlier if j < DIRECT_FROM else has_earlier)(backs[j].start)
        if 0 < j < DIRECT_FROM:
            pl.when(far_earlier)(edges[j].start)
        acc[j, 0] = dk[TQ:]
        acc[j, 1] = dv[TQ:]

    def finish(j):
        @pl.when(near_later if j < DIRECT_FROM else has_later)
        def _():
            backs[j].wait_recv()
            acc[j] += back_in[j].astype(jnp.float32)

        if j > 0:
            part_out[j] = acc[j].astype(jnp.bfloat16)
            parts[j].start()

    def pass_on(j):
        gathers[j].wait_recv()
        pl.when(near_later)(forwards[j].start)

    @pl.when(eager)
    def _():
        for j in steps[1:]:
            pass_on(j)
        for j in steps:
            own_block(j)

    @pl.when(jnp.logical_not(has_earlier))
    def _():
        prev[...] = jnp.zeros_like(prev)

    @pl.when(far_earlier)
    def _():
        forwards[0].wait_recv()
        for j in steps[1:]:
            relays[j].start()

    @pl.when(steady)
    def _():
        for j in range(1, AHEAD):
            pass_on(j)

    pl.when(near_earlier)(forwards[0].wait_recv)

    for j in steps:
        if AHEAD <= j + AHEAD < KV_HEADS:
            pl.when(steady)(functools.partial(pass_on, j + AHEAD))
        pl.when(steady)(functools.partial(own_block, j))
        if j > 0:
            pl.when(has_earlier)(forwards[j].wait_recv)
        compute(j)
        pl.when(eager)(functools.partial(finish, j))
        if j >= LAG:
            pl.when(steady)(functools.partial(finish, j - LAG))
    for j in range(KV_HEADS - LAG, KV_HEADS):
        pl.when(steady)(functools.partial(finish, j))

    @pl.when(far_earlier)
    def _():
        total = back_out[0].astype(jnp.float32)
        for j in range(1, DIRECT_FROM):
            edges[j].wait_recv()
            total = total + edge_in[j].astype(jnp.float32)
        edge_out[...] = total.astype(jnp.bfloat16)
        edges[0].start()

    total = acc[0]
    for j in steps[1:]:
        parts[j].wait_recv()
        total = total + part_in[j].astype(jnp.float32)
    dkv_ref[...] = total

    @pl.when(far_later)
    def _():
        edges[0].wait_recv()
        dkv_ref[...] += edge_last[...].astype(jnp.float32)

    pl.when(near_later)(forwards[0].wait_send)
    for j in steps:
        pl.when(near_earlier if j < DIRECT_FROM else has_earlier)(backs[j].wait_send)
        if j < DIRECT_FROM:
            pl.when(far_earlier)(edges[j].wait_send)
        if j > 0:
            gathers[j].wait_send()
            parts[j].wait_send()
            pl.when(near_later)(forwards[j].wait_send)
            pl.when(far_earlier)(relays[j].wait_send)


def body(queries, grad_out, keys, values, key_first):
    rows, width = queries.shape[1:]
    block = (KV_HEADS, 2, TQ, HEAD_DIM)
    group = (KV_HEADS, rows, GROUP_WIDTH)
    pairs = math.prod((KV_HEADS, GROUP, TQ, 2 * TQ))
    grad_queries, cache_grads = pl.pallas_call(
        kernel,
        out_shape=(
            pltpu.VMEM(queries.shape, jnp.bfloat16),
            pltpu.VMEM((2,) + keys.shape, jnp.float32),
        ),
        in_specs=[pl.BlockSpec(memory_space=pltpu.HBM)] * 5,
        out_specs=[pl.BlockSpec(memory_space=pltpu.VMEM)] * 2,
        scratch_shapes=[
            pltpu.VMEM(group, jnp.bfloat16),
            pltpu.VMEM(group, jnp.bfloat16),
            pltpu.VMEM(block, jnp.bfloat16),
            pltpu.VMEM(block, jnp.bfloat16),
            pltpu.VMEM(block, jnp.float32),
            pltpu.VMEM(block, jnp.bfloat16),
            pltpu.VMEM(block, jnp.bfloat16),
            pltpu.VMEM(block, jnp.bfloat16),
            pltpu.VMEM(block, jnp.bfloat16),
            pltpu.VMEM(block, jnp.bfloat16),
            pltpu.VMEM(block[1:], jnp.bfloat16),
            pltpu.VMEM(block[1:], jnp.bfloat16),
            pltpu.VMEM((KV_HEADS, TQ, GROUP * rows), jnp.float32),
            pltpu.VMEM((KV_HEADS, TQ, GROUP * rows), jnp.float32),
            pltpu.VMEM((KV_HEADS, 8, GROUP * rows), jnp.float32),
            pltpu.SMEM((1,), jnp.int32),
            pltpu.SemaphoreType.DMA((KV_HEADS,)),
            pltpu.SemaphoreType.DMA((KV_HEADS,)),
            pltpu.SemaphoreType.DMA((2,)),
            pltpu.SemaphoreType.DMA,
        ]
        + [pltpu.SemaphoreType.DMA((KV_HEADS,))] * 11,
        compiler_params=pltpu.CompilerParams(
            collective_id=0, has_side_effects=True, vmem_limit_bytes=56 * 2**20
        ),
        cost_estimate=pl.CostEstimate(
            flops=10 * pairs * HEAD_DIM, transcendentals=pairs, bytes_accessed=3 * 2 * rows * width
        ),
    )(queries, grad_out, keys, values, key_first)
    return grad_queries, cache_grads[0], cache_grads[1]


def solution(mesh):
    placed = (
        P("section", "seq", None),
        P("section", "seq", None),
        P("seq", "section"),
        P("seq", "section"),
        P("seq"),
    )
    return jax.shard_map(
        body,
        mesh=mesh,
        in_specs=placed,
        out_specs=(P("section", "seq", None), P("seq", "section"), P("seq", "section")),
        check_vma=False,
    )
```
